32 devices in a mesh: dp: 8 (over y, x, core), tensor: 4 (over z).
Axes of the slice: x: 2, y: 2, z: 4, core: 2. Of those that a mesh axis runs over, the one named last changes fastest.
Arguments:
- block_input: bfloat16 [4096, 1024], P(('dp', 'tensor')), may hold values from -6 to 6
- first_gain: bfloat16 [1024], P('dp'), may hold values from 0.25 to 1.75
- query_gain: bfloat16 [128], P('dp'), may hold values from 0.25 to 1.75
- key_gain: bfloat16 [128], P('dp'), may hold values from 0.25 to 1.75
- query_weight: bfloat16 [1024, 2048], P('dp', 'tensor'), may hold values from -0.1875 to 0.1875
- key_matrix: bfloat16 [1024, 1024], P('dp', 'tensor'), may hold values from -0.1875 to 0.1875
- value_matrix: bfloat16 [1024, 1024], P('dp', 'tensor'), may hold values from -0.1875 to 0.1875
- output_weight: bfloat16 [2048, 1024], P('tensor', 'dp'), may hold values from -0.5 to 0.5
- second_gain: bfloat16 [1024], P('dp'), may hold values from 0.25 to 1.75
- gate_weight: bfloat16 [1024, 3072], P('dp', 'tensor'), may hold values from -0.1875 to 0.1875
- up_weight: bfloat16 [1024, 3072], P('dp', 'tensor'), may hold values from -0.1875 to 0.1875
- down_weight: bfloat16 [3072, 1024], P('tensor', 'dp'), may hold values from -0.109375 to 0.109375
- out_grad: bfloat16 [4096, 1024], P(('dp', 'tensor')), may hold values from -6 to 6
Outputs:
- block_output: bfloat16 [4096, 1024], P(('dp', 'tensor'))
- input_grad: float32 [4096, 1024], P(('dp', 'tensor'))
- first_gain_grad: float32 [1024], P('dp')
- query_gain_grad: float32 [128], P('dp')
- key_gain_grad: float32 [128], P('dp')
- query_weight_grad: float32 [1024, 2048], P('dp', 'tensor')
- key_weight_grad: float32 [1024, 1024], P('dp', 'tensor')
- value_weight_grad: float32 [1024, 1024], P('dp', 'tensor')
- output_weight_grad: float32 [2048, 1024], P('tensor', 'dp')
- second_gain_grad: float32 [1024], P('dp')
- gate_weight_grad: float32 [1024, 3072], P('dp', 'tensor')
- up_weight_grad: float32 [1024, 3072], P('dp', 'tensor')
- down_weight_grad: float32 [3072, 1024], P('tensor', 'dp')
The draws below stay inside these ranges and needn't reach their ends.
All inputs are finite; a program needn't handle non-finite values.
Results may differ from the reference program's by a relative error of at most 0.017.
Values may be sent and summed in bfloat16 or wider, within the bound.
No kernel may reach another device: no remote copies, remote signals or barrier semaphores. Data moves between devices by JAX's collectives and lax.ppermute only.
A program may use at most 128 MiB of HBM per device.

```python
import jax
import jax.numpy as jnp
from jax import lax

MODEL_WIDTH = 1024
FEED_HIDDEN = 3072
QUERY_HEADS = 16
KEY_VALUE_HEADS = 8
HEAD_SIZE = 128
LEN = 512
TOKENS = 4096
N_DP = 8


def block_scale(rng, extent, split, smallest, high):
    loudness, own = 1.0, jax.random.fold_in(rng, 6)
    for axis_at, shards_of in split:
        steps = jnp.exp(jax.random.uniform(jax.random.fold_in(own, axis_at), (shards_of,), jnp.float32, smallest / len(split), high / len(split)))
        loudness = loudness * jnp.repeat(steps, extent[axis_at] // shards_of).reshape([-1 if axis == axis_at else 1 for axis in range(len(extent))])
    return loudness


def centred(stream_key, shape, scale, limit, shards=(), kind=jnp.bfloat16):
    values = scale * jax.random.normal(stream_key, shape, jnp.float32)
    if shards:
        values = values * block_scale(stream_key, shape, shards, -0.22, 0.18)
    return jnp.clip(values, -limit, limit).astype(kind)


def setup_inputs(seed: int = 0) -> dict:
    key_of = jax.random.split(jax.random.key(seed), 14)
    block_input = centred(key_of[0], (TOKENS, MODEL_WIDTH), 1.0, 6.0, ((0, 32),))
    first_gain = jnp.clip(1.0 + 0.15 * jax.random.normal(key_of[1], (MODEL_WIDTH,), jnp.float32), 0.25, 1.75).astype(jnp.bfloat16)
    query_gain = jnp.clip(1.0 + 0.15 * jax.random.normal(key_of[2], (HEAD_SIZE,), jnp.float32), 0.25, 1.75).astype(jnp.bfloat16)
    key_gain = jnp.clip(1.0 + 0.15 * jax.random.normal(key_of[3], (HEAD_SIZE,), jnp.float32), 0.25, 1.75).astype(jnp.bfloat16)
    query_weight = centred(key_of[4], (MODEL_WIDTH, QUERY_HEADS * HEAD_SIZE), MODEL_WIDTH ** -0.5, 0.1875, ((0, 8), (1, 4)))
    key_matrix = centred(key_of[5], (MODEL_WIDTH, KEY_VALUE_HEADS * HEAD_SIZE), MODEL_WIDTH ** -0.5, 0.1875, ((0, 8), (1, 4)))
    value_matrix = centred(key_of[6], (MODEL_WIDTH, KEY_VALUE_HEADS * HEAD_SIZE), MODEL_WIDTH ** -0.5, 0.1875, ((0, 8), (1, 4)))
    output_weight = centred(key_of[7], (QUERY_HEADS * HEAD_SIZE, MODEL_WIDTH), HEAD_SIZE ** -0.5, 0.5, ((0, 4), (1, 8)))
    second_gain = jnp.clip(1.0 + 0.15 * jax.random.normal(key_of[8], (MODEL_WIDTH,), jnp.float32), 0.25, 1.75).astype(jnp.bfloat16)
    gate_weight = centred(key_of[9], (MODEL_WIDTH, FEED_HIDDEN), MODEL_WIDTH ** -0.5, 0.1875, ((0, 8), (1, 4)))
    up_weight = centred(key_of[10], (MODEL_WIDTH, FEED_HIDDEN), MODEL_WIDTH ** -0.5, 0.1875, ((0, 8), (1, 4)))
    down_weight = centred(key_of[11], (FEED_HIDDEN, MODEL_WIDTH), FEED_HIDDEN ** -0.5, 0.109375, ((0, 4), (1, 8)))
    out_grad = centred(key_of[12], (TOKENS, MODEL_WIDTH), 1.0, 6.0, ((0, 32),))
    return dict(block_input=block_input, first_gain=first_gain, query_gain=query_gain, key_gain=key_gain, query_weight=query_weight, key_matrix=key_matrix, value_matrix=value_matrix, output_weight=output_weight, second_gain=second_gain, gate_weight=gate_weight, up_weight=up_weight, down_weight=down_weight, out_grad=out_grad)


EPSILON = 1e-06
THETA = 1000000.0

def rope_tables(length, width):
    half = width // 2
    freqs = THETA ** (-(jnp.arange(half, dtype=jnp.float32) * (2.0 / width)))
    angles = jnp.arange(length, dtype=jnp.float32)[:, None] * freqs[None, :]
    angles = jnp.concatenate([angles, angles], axis=1)
    return (jnp.cos(angles), jnp.sin(angles))

def rotate_half(values):
    half = values.shape[-1] // 2
    return jnp.concatenate([-values[..., half:], values[..., :half]], axis=-1)

def rotate_back(values):
    half = values.shape[-1] // 2
    return jnp.concatenate([values[..., half:], -values[..., :half]], axis=-1)

def apply_rope(values, cosine, sine):
    return values * cosine[:, None, :] + rotate_half(values) * sine[:, None, :]

def rope_back(grads, cosine, sine):
    return grads * cosine[:, None, :] + rotate_back(grads * sine[:, None, :])

def row_norm(rows, gain):
    inverse = lax.rsqrt(lax.optimization_barrier(jnp.mean(rows * rows, axis=-1, keepdims=True)) + EPSILON)
    normed = rows * inverse
    return (inverse, normed, (normed * gain.astype(jnp.float32)).astype(jnp.bfloat16))

def norm_back(grads, inverse, normed, gain):
    scaled = grads * gain.astype(jnp.float32)
    inner = lax.optimization_barrier(jnp.mean(scaled * normed, axis=-1, keepdims=True))
    return inverse * (scaled - normed * inner)

def head_prepare(raw, gain, cosine, sine):
    inverse = lax.rsqrt(lax.optimization_barrier(jnp.mean(raw * raw, axis=-1, keepdims=True)) + EPSILON)
    hat = raw * inverse
    rotated = apply_rope(hat * gain.astype(jnp.float32), cosine, sine).astype(jnp.bfloat16)
    return (inverse, hat, rotated)

def head_back(grad_rot, inverse, hat, gain, cosine, sine):
    grad_normed = rope_back(grad_rot, cosine, sine)
    gain_grad = lax.optimization_barrier(jnp.sum(grad_normed * hat, axis=(0, 1)))
    return (norm_back(grad_normed, inverse, hat, gain), gain_grad)

def causal_scores(queries, keys, scale):
    length = queries.shape[0]
    scores = jnp.einsum('qkgd,skd->kgqs', queries.astype(jnp.float32), keys.astype(jnp.float32)) * scale
    row_index = lax.broadcasted_iota(jnp.int32, (length, length), 0)
    col_index = lax.broadcasted_iota(jnp.int32, (length, length), 1)
    return jnp.where(row_index >= col_index, scores, -1e+30)

def attend(queries, keys, values, scale):
    scores = causal_scores(queries, keys, scale)
    totals = jax.nn.logsumexp(scores, axis=-1)
    probs = jnp.exp(scores - totals[..., None]).astype(jnp.bfloat16)
    result = jnp.einsum('kgqs,skd->qkgd', probs.astype(jnp.float32), values.astype(jnp.float32))
    return (result.astype(jnp.bfloat16), totals)

def attend_back(queries, keys, values, attended, grad_attended, totals, scale):
    scores = causal_scores(queries, keys, scale)
    probs = jnp.exp(scores - totals[..., None])
    probs_low = probs.astype(jnp.bfloat16).astype(jnp.float32)
    grad_f = grad_attended.astype(jnp.float32)
    grad_probs = jnp.einsum('qkgd,skd->kgqs', grad_f, values.astype(jnp.float32))
    delta = jnp.einsum('qkgd,qkgd->kgq', grad_f, attended.astype(jnp.float32))
    grad_scores = (probs * (grad_probs - delta[..., None]) * scale).astype(jnp.bfloat16).astype(jnp.float32)
    grad_query = jnp.einsum('kgqs,skd->qkgd', grad_scores, keys.astype(jnp.float32))
    grad_key = jnp.einsum('kgqs,qkgd->skd', grad_scores, queries.astype(jnp.float32))
    grad_value = jnp.einsum('kgqs,qkgd->skd', probs_low, grad_f)
    return (grad_query, grad_key, grad_value)

def layer_sequence(rows_in, grad_out, params):
    gain_one, gain_query, gain_key, query_full, key_full, value_full, output_full, gain_two, gate_full, up_full, down_full = params
    length = rows_in.shape[0]
    head_dim = gain_query.shape[0]
    query_heads = query_full.shape[1] // head_dim
    kv_heads = key_full.shape[1] // head_dim
    group = query_heads // kv_heads
    scale = head_dim ** (-0.5)
    cosine, sine = rope_tables(length, head_dim)
    input_float = rows_in.astype(jnp.float32)
    inverse_one, normed_one, hidden_one = row_norm(input_float, gain_one)
    query_raw = jnp.dot(hidden_one, query_full, preferred_element_type=jnp.float32).reshape(length, query_heads, head_dim)
    key_raw = jnp.dot(hidden_one, key_full, preferred_element_type=jnp.float32).reshape(length, kv_heads, head_dim)
    value_rows = jnp.dot(hidden_one, value_full, preferred_element_type=jnp.float32).astype(jnp.bfloat16).reshape(length, kv_heads, head_dim)
    query_inverse, query_hat, query_rot = head_prepare(query_raw, gain_query, cosine, sine)
    key_inverse, key_hat, key_rot = head_prepare(key_raw, gain_key, cosine, sine)
    query_grouped = query_rot.reshape(length, kv_heads, group, head_dim)
    attended, totals = attend(query_grouped, key_rot, value_rows, scale)
    attended_flat = attended.reshape(length, query_heads * head_dim)
    middle = input_float + jnp.dot(attended_flat, output_full, preferred_element_type=jnp.float32)
    inverse_two, normed_two, hidden_two = row_norm(middle, gain_two)
    gate_rows = jnp.dot(hidden_two, gate_full, preferred_element_type=jnp.float32)
    up_rows = jnp.dot(hidden_two, up_full, preferred_element_type=jnp.float32)
    sigmoid_gate = jax.nn.sigmoid(gate_rows)
    silu_gate = gate_rows * sigmoid_gate
    mixed = (silu_gate * up_rows).astype(jnp.bfloat16)
    block_output = (middle + jnp.dot(mixed, down_full, preferred_element_type=jnp.float32)).astype(jnp.bfloat16)
    grad_mixed = jnp.dot(grad_out, down_full.T, preferred_element_type=jnp.float32)
    down_grad = jnp.dot(mixed.T, grad_out, preferred_element_type=jnp.float32)
    derivative = sigmoid_gate * (1.0 + gate_rows * (1.0 - sigmoid_gate))
    grad_gate = (grad_mixed * up_rows * derivative).astype(jnp.bfloat16)
    grad_up = (grad_mixed * silu_gate).astype(jnp.bfloat16)
    gate_grad = jnp.dot(hidden_two.T, grad_gate, preferred_element_type=jnp.float32)
    up_grad = jnp.dot(hidden_two.T, grad_up, preferred_element_type=jnp.float32)
    hidden_two_grad = jnp.dot(grad_gate, gate_full.T, preferred_element_type=jnp.float32) + jnp.dot(grad_up, up_full.T, preferred_element_type=jnp.float32)
    gain_two_grad = lax.optimization_barrier(jnp.sum(hidden_two_grad * normed_two, axis=0))
    middle_grad = grad_out.astype(jnp.float32) + norm_back(hidden_two_grad, inverse_two, normed_two, gain_two)
    grad_attn = middle_grad.astype(jnp.bfloat16)
    output_grad_w = jnp.dot(attended_flat.T, grad_attn, preferred_element_type=jnp.float32)
    grad_attended = jnp.dot(grad_attn, output_full.T, preferred_element_type=jnp.float32).astype(jnp.bfloat16)
    grad_query_rot, grad_key_rot, grad_value = attend_back(query_grouped, key_rot, value_rows, attended, grad_attended.reshape(length, kv_heads, group, head_dim), totals, scale)
    grad_query_raw, query_gain_grad = head_back(grad_query_rot.reshape(length, query_heads, head_dim), query_inverse, query_hat, gain_query, cosine, sine)
    grad_key_raw, key_gain_grad = head_back(grad_key_rot, key_inverse, key_hat, gain_key, cosine, sine)
    grad_query = grad_query_raw.reshape(length, query_heads * head_dim).astype(jnp.bfloat16)
    grad_key = grad_key_raw.reshape(length, kv_heads * head_dim).astype(jnp.bfloat16)
    grad_val = grad_value.reshape(length, kv_heads * head_dim).astype(jnp.bfloat16)
    query_grad_w = jnp.dot(hidden_one.T, grad_query, preferred_element_type=jnp.float32)
    key_grad_w = jnp.dot(hidden_one.T, grad_key, preferred_element_type=jnp.float32)
    value_grad_w = jnp.dot(hidden_one.T, grad_val, preferred_element_type=jnp.float32)
    hidden_one_grad = jnp.dot(grad_query, query_full.T, preferred_element_type=jnp.float32) + jnp.dot(grad_key, key_full.T, preferred_element_type=jnp.float32) + jnp.dot(grad_val, value_full.T, preferred_element_type=jnp.float32)
    gain_one_grad = lax.optimization_barrier(jnp.sum(hidden_one_grad * normed_one, axis=0))
    input_grad = middle_grad + norm_back(hidden_one_grad, inverse_one, normed_one, gain_one)
    grads = (gain_one_grad, query_gain_grad, key_gain_grad, query_grad_w, key_grad_w, value_grad_w, output_grad_w, gain_two_grad, gate_grad, up_grad, down_grad)
    return (block_output, input_grad, grads)

def reference(block_input, first_gain, query_gain, key_gain, query_weight, key_matrix, value_matrix, output_weight, second_gain, gate_weight, up_weight, down_weight, out_grad):
    params = (first_gain, query_gain, key_gain, query_weight, key_matrix, value_matrix, output_weight, second_gain, gate_weight, up_weight, down_weight)
    inputs_seq = block_input.reshape(N_DP, LEN, MODEL_WIDTH)
    grads_seq = out_grad.reshape(N_DP, LEN, MODEL_WIDTH)
    zero_filled = (jnp.zeros((MODEL_WIDTH,), jnp.float32), jnp.zeros((HEAD_SIZE,), jnp.float32), jnp.zeros((HEAD_SIZE,), jnp.float32), jnp.zeros((MODEL_WIDTH, QUERY_HEADS * HEAD_SIZE), jnp.float32), jnp.zeros((MODEL_WIDTH, KEY_VALUE_HEADS * HEAD_SIZE), jnp.float32), jnp.zeros((MODEL_WIDTH, KEY_VALUE_HEADS * HEAD_SIZE), jnp.float32), jnp.zeros((QUERY_HEADS * HEAD_SIZE, MODEL_WIDTH), jnp.float32), jnp.zeros((MODEL_WIDTH,), jnp.float32), jnp.zeros((MODEL_WIDTH, FEED_HIDDEN), jnp.float32), jnp.zeros((MODEL_WIDTH, FEED_HIDDEN), jnp.float32), jnp.zeros((FEED_HIDDEN, MODEL_WIDTH), jnp.float32))

    def step(carry, pair):
        block_out, input_g, grads = layer_sequence(pair[0], pair[1], params)
        return (tuple((total + part for total, part in zip(carry, grads))), (block_out, input_g))
    totals, (outputs, input_grads) = lax.scan(step, zero_filled, (inputs_seq, grads_seq))
    return (outputs.reshape(TOKENS, MODEL_WIDTH), input_grads.reshape(TOKENS, MODEL_WIDTH), totals[0], totals[1], totals[2], totals[3], totals[4], totals[5], totals[6], totals[7], totals[8], totals[9], totals[10])
```

```python
import jax
import jax.numpy as jnp
from jax import lax
from jax.sharding import PartitionSpec as P

EPSILON = 1e-06
THETA = 1000000.0
LOW = jnp.bfloat16
WIDE = jnp.float32


def send(values, axis, bit):
    size = lax.axis_size(axis)
    return lax.ppermute(values, axis, [(i, i ^ bit) for i in range(size)])


def halves(rows):
    middle = rows.shape[0] // 2
    return (rows[:middle], rows[middle:])


def gather_rows(shard):
    size = lax.axis_size("dp")
    if size == 8:
        from_x = send(shard, "dp", 2)
        from_y = send(shard, "dp", 4)
        first = send(halves(from_x)[0], "dp", 4)
        second = send(halves(from_y)[1], "dp", 2)
        own = jnp.concatenate([shard, from_x, from_y, first, second], axis=0)
    else:
        own = shard
        bit = 2
        while bit < size:
            own = jnp.concatenate([own, send(own, "dp", bit)], axis=0)
            bit *= 2
    return (own, send(own, "dp", 1))


def scatter_rows(own, other):
    size = lax.axis_size("dp")
    own = own + send(other.astype(LOW), "dp", 1).astype(WIDE)
    if size == 8:
        here, to_x, to_y, far = jnp.split(own, 4, axis=0)
        far_x, far_y = halves(far.astype(LOW))
        by_x = send(far_x, "dp", 2).astype(WIDE)
        by_y = send(far_y, "dp", 4).astype(WIDE)
        x_low, x_high = halves(to_x)
        y_low, y_high = halves(to_y)
        to_x = jnp.concatenate([x_low, x_high + by_y], axis=0).astype(LOW)
        to_y = jnp.concatenate([y_low + by_x, y_high], axis=0).astype(LOW)
        return here + send(to_x, "dp", 2).astype(WIDE) + send(to_y, "dp", 4).astype(WIDE)
    bit = size // 2
    while bit > 1:
        low, high = halves(own)
        own = low + send(high.astype(LOW), "dp", bit).astype(WIDE)
        bit //= 2
    return own


def swap_blocks(rows, block_of):
    size = lax.axis_size("dp")
    width = rows.shape[-1] // size
    index = lax.axis_index("dp")
    blocks = [rows[..., i * width : (i + 1) * width] for i in range(size)]
    bit = 1
    while bit < size:
        taken = (index & bit) != 0
        blocks = [jnp.where(taken, blocks[i ^ bit], blocks[i]) for i in range(size)]
        bit *= 2
    return jnp.concatenate([blocks[i] for i in block_of], axis=-1)


def to_relative(rows):
    size = lax.axis_size("dp")
    return swap_blocks(rows, [2 * i for i in range(size // 2)] + [2 * i + 1 for i in range(size // 2)])


def to_absolute(rows):
    size = lax.axis_size("dp")
    width = rows.shape[-1] // size
    index = lax.axis_index("dp")
    order = [2 * i for i in range(size // 2)] + [2 * i + 1 for i in range(size // 2)]
    place = [order.index(i) for i in range(size)]
    blocks = [rows[..., i * width : (i + 1) * width] for i in place]
    bit = 1
    while bit < size:
        taken = (index & bit) != 0
        blocks = [jnp.where(taken, blocks[i ^ bit], blocks[i]) for i in range(size)]
        bit *= 2
    return jnp.concatenate(blocks, axis=-1)


def gather_tokens(rows):
    size = lax.axis_size("tensor")
    return jnp.concatenate([rows] + [send(rows, "tensor", k) for k in range(1, size)], axis=0)


def scatter_tokens(parts):
    total = parts[0]
    for k in range(1, len(parts)):
        total = total + send(parts[k].astype(LOW), "tensor", k).astype(WIDE)
    return total


def sum_tensor(values):
    size = lax.axis_size("tensor")
    total = values
    for k in range(1, size):
        total = total + send(values, "tensor", k)
    return total


def sum_all(values):
    for axis in ("dp", "tensor"):
        bit = 1
        while bit < lax.axis_size(axis):
            values = values + send(values, axis, bit)
            bit *= 2
    return values


def gather_small(values):
    size = lax.axis_size("dp")
    index = lax.axis_index("dp")
    count = values.shape[0]
    place = lax.broadcasted_iota(jnp.int32, (size, count), 0) == index
    full = jnp.where(place, values[None, :], jnp.zeros_like(values)[None, :])
    bit = 1
    while bit < size:
        full = full + send(full, "dp", bit)
        bit *= 2
    return full


def rotate_half(values):
    half = values.shape[-1] // 2
    return jnp.concatenate([-values[..., half:], values[..., :half]], axis=-1)


def rotate_back(values):
    half = values.shape[-1] // 2
    return jnp.concatenate([values[..., half:], -values[..., :half]], axis=-1)


def dot(left, right):
    return lax.dot_general(left, right, (((1,), (0,)), ((), ())), preferred_element_type=WIDE)


def dot_rows(left, right):
    return lax.dot_general(left, right, (((0,), (0,)), ((), ())), preferred_element_type=WIDE)


def dot_columns(left, right):
    return lax.dot_general(left, right, (((1,), (1,)), ((), ())), preferred_element_type=WIDE)


def normalise(rows):
    inverse = lax.rsqrt(jnp.mean(rows * rows, axis=-1, keepdims=True) + EPSILON)
    return (inverse, rows * inverse)


def norm_back(scaled, inverse, normed):
    inner = jnp.mean(scaled * normed, axis=-1, keepdims=True)
    return inverse * (scaled - normed * inner)


def weight_grad(rows, grads):
    half = rows.shape[1] // 2
    return (dot_rows(rows[:, :half], grads), dot_rows(rows[:, half:], grads).astype(LOW))


def body(
    block_input,
    first_gain,
    query_gain,
    key_gain,
    query_weight,
    key_matrix,
    value_matrix,
    output_weight,
    second_gain,
    gate_weight,
    up_weight,
    down_weight,
    out_grad,
):
    ranks = lax.axis_size("tensor")
    rank = lax.axis_index("tensor")
    dp_size = lax.axis_size("dp")
    dp_index = lax.axis_index("dp")
    local = block_input.shape[0]
    length = local * ranks
    head_dim = query_gain.shape[0] * dp_size
    query_width = query_weight.shape[1]
    key_width = key_matrix.shape[1]
    query_heads = query_width // head_dim
    kv_heads = key_width // head_dim
    group = query_heads // kv_heads
    hidden = gate_weight.shape[1]
    scale = head_dim ** (-0.5)

    gain_one = first_gain.astype(WIDE)[:, None]
    gain_two = second_gain.astype(WIDE)[:, None]
    in_local = jnp.concatenate([query_weight, key_matrix, value_matrix], axis=1)
    in_shard = (in_local.astype(WIDE) * gain_one).astype(LOW)
    out_shard = output_weight.T
    feed_local = jnp.concatenate([gate_weight, up_weight], axis=1)
    feed_shard = (feed_local.astype(WIDE) * gain_two).astype(LOW)
    down_shard = down_weight.T

    in_full = jnp.concatenate(gather_rows(in_shard), axis=0)
    input_float = to_relative(block_input).astype(WIDE)
    inverse_one, normed_one = normalise(input_float)
    rows_one = gather_tokens(normed_one.astype(LOW))
    gains = gather_small(jnp.concatenate([query_gain, key_gain])).astype(WIDE)
    small = query_gain.shape[0]
    gain_query = gains[:, :small].reshape(-1)
    gain_key = gains[:, small:].reshape(-1)
    out_full = jnp.concatenate(gather_rows(out_shard), axis=0)
    grad_local = to_relative(out_grad)
    grad_rows = gather_tokens(grad_local)
    feed_full = jnp.concatenate(gather_rows(feed_shard), axis=0)
    down_full = jnp.concatenate(gather_rows(down_shard), axis=0)

    slot = lax.broadcasted_iota(jnp.int32, (ranks, local), 0)
    within = lax.broadcasted_iota(jnp.int32, (ranks, local), 1)
    position = ((slot ^ rank) * local + within).reshape(length)
    half = head_dim // 2
    freqs = THETA ** (-(jnp.arange(half, dtype=WIDE) * (2.0 / head_dim)))
    angles = position.astype(WIDE)[:, None] * freqs[None, :]
    angles = jnp.concatenate([angles, angles], axis=1)
    cosine = jnp.cos(angles)[:, None, :]
    sine = jnp.sin(angles)[:, None, :]
    visible = position[:, None] >= position[None, :]

    def prepare(raw, gain):
        inverse = lax.rsqrt(jnp.mean(raw * raw, axis=-1, keepdims=True) + EPSILON)
        hat = raw * inverse
        scaled = hat * gain
        return (inverse, hat, (scaled * cosine + rotate_half(scaled) * sine).astype(LOW))

    def prepare_back(grad_rot, inverse, hat, gain):
        grad_normed = grad_rot * cosine + rotate_back(grad_rot * sine)
        gain_grad = jnp.sum(grad_normed * hat, axis=(0, 1))
        scaled = grad_normed * gain
        inner = jnp.mean(scaled * hat, axis=-1, keepdims=True)
        return (inverse * (scaled - hat * inner), gain_grad)

    projected = dot(rows_one, in_full)
    query_raw = projected[:, :query_width].reshape(length, query_heads, head_dim)
    key_raw = projected[:, query_width : query_width + key_width].reshape(length, kv_heads, head_dim)
    values = projected[:, query_width + key_width :].astype(LOW).reshape(length, kv_heads, head_dim)
    query_inverse, query_hat, query_rot = prepare(query_raw, gain_query)
    key_inverse, key_hat, keys = prepare(key_raw, gain_key)
    queries = query_rot.reshape(length, kv_heads, group, head_dim)

    scores = jnp.einsum("qkgd,skd->kgqs", queries, keys, preferred_element_type=WIDE) * scale
    scores = jnp.where(visible, scores, -1e30)
    totals = jax.nn.logsumexp(scores, axis=-1)
    probs = jnp.exp(scores - totals[..., None])
    probs_low = probs.astype(LOW)
    attended = jnp.einsum("kgqs,skd->qkgd", probs_low, values, preferred_element_type=WIDE).astype(LOW)
    attended_flat = attended.reshape(length, query_width)
    attention_part = dot_columns(attended_flat, out_full)
    middle = input_float + scatter_tokens(jnp.split(attention_part, ranks, axis=0))

    inverse_two, normed_two = normalise(middle)
    rows_two = gather_tokens(normed_two.astype(LOW))
    gate_up = dot(rows_two, feed_full)
    gate_rows, up_rows = gate_up[:, :hidden], gate_up[:, hidden:]
    sigmoid_gate = jax.nn.sigmoid(gate_rows)
    silu_gate = gate_rows * sigmoid_gate
    mixed = (silu_gate * up_rows).astype(LOW)
    grad_mixed = dot(grad_rows, down_full)
    derivative = sigmoid_gate * (1.0 + gate_rows * (1.0 - sigmoid_gate))
    grad_gate = (grad_mixed * up_rows * derivative).astype(LOW)
    grad_up = (grad_mixed * silu_gate).astype(LOW)
    grad_gate_up = jnp.concatenate([grad_gate, grad_up], axis=1)
    second_part = dot_columns(grad_gate_up, feed_full)
    scaled_two = scatter_tokens(jnp.split(second_part, ranks, axis=0))
    middle_grad = grad_local.astype(WIDE) + norm_back(scaled_two, inverse_two, normed_two)
    grad_attn = gather_tokens(middle_grad.astype(LOW))

    feed_part = dot_columns(mixed, down_full)
    block_output = middle + scatter_tokens(jnp.split(feed_part, ranks, axis=0))
    block_output = to_absolute(block_output.astype(LOW))
    feed_total = scatter_rows(*weight_grad(rows_two, grad_gate_up))
    down_total = scatter_rows(*weight_grad(grad_rows, mixed))
    feed_grad = feed_total * gain_two
    second_gain_grad = sum_tensor(jnp.sum(feed_total * feed_local.astype(WIDE), axis=1))

    out_total = scatter_rows(*weight_grad(grad_attn, attended_flat))
    grad_attended = dot(grad_attn, out_full).astype(LOW).reshape(length, kv_heads, group, head_dim)
    grad_probs = jnp.einsum("qkgd,skd->kgqs", grad_attended, values, preferred_element_type=WIDE)
    delta = jnp.einsum("qkgd,qkgd->kgq", grad_attended.astype(WIDE), attended.astype(WIDE))
    grad_scores = (probs * (grad_probs - delta[..., None]) * scale).astype(LOW)
    grad_query_rot = jnp.einsum("kgqs,skd->qkgd", grad_scores, keys, preferred_element_type=WIDE)
    grad_key_rot = jnp.einsum("kgqs,qkgd->skd", grad_scores, queries, preferred_element_type=WIDE)
    grad_value = jnp.einsum("kgqs,qkgd->skd", probs_low, grad_attended, preferred_element_type=WIDE)
    grad_query, query_part = prepare_back(
        grad_query_rot.reshape(length, query_heads, head_dim), query_inverse, query_hat, gain_query
    )
    grad_key, key_part = prepare_back(grad_key_rot, key_inverse, key_hat, gain_key)
    grad_in = jnp.concatenate(
        [
            grad_query.reshape(length, query_width).astype(LOW),
            grad_key.reshape(length, key_width).astype(LOW),
            grad_value.reshape(length, key_width).astype(LOW),
        ],
        axis=1,
    )
    first_part = dot_columns(grad_in, in_full)
    scaled_one = scatter_tokens(jnp.split(first_part, ranks, axis=0))
    in_total = scatter_rows(*weight_grad(rows_one, grad_in))
    input_grad = to_absolute(middle_grad + norm_back(scaled_one, inverse_one, normed_one))
    head_gains = sum_all(jnp.concatenate([query_part, key_part]))
    query_gain_grad = lax.dynamic_slice(head_gains, (dp_index * small,), (small,))
    key_gain_grad = lax.dynamic_slice(head_gains, (head_dim + dp_index * small,), (small,))
    in_grad = in_total * gain_one
    first_gain_grad = sum_tensor(jnp.sum(in_total * in_local.astype(WIDE), axis=1))

    return (
        block_output,
        input_grad,
        first_gain_grad,
        query_gain_grad,
        key_gain_grad,
        in_grad[:, :query_width],
        in_grad[:, query_width : query_width + key_width],
        in_grad[:, query_width + key_width :],
        out_total.T,
        second_gain_grad,
        feed_grad[:, :hidden],
        feed_grad[:, hidden:],
        down_total.T,
    )


def solution(mesh):
    tokens = P(("dp", "tensor"), None)
    vector = P("dp")
    rows = P("dp", "tensor")
    columns = P("tensor", "dp")
    return jax.shard_map(
        body,
        mesh=mesh,
        in_specs=(tokens, vector, vector, vector, rows, rows, rows, columns, vector, rows, rows, columns, tokens),
        out_specs=(tokens, tokens, vector, vector, vector, rows, rows, rows, columns, vector, rows, rows, columns),
        check_vma=False,
    )
```

```python
import functools

import jax
import jax.numpy as jnp
from jax import lax
from jax.experimental import pallas as pl
from jax.experimental.pallas import tpu as pltpu
from jax.sharding import PartitionSpec as P

EPSILON = 1e-06
THETA = 1000000.0
LOW = jnp.bfloat16
WIDE = jnp.float32
TILE = 256
HIDDEN_FAR = -1e30


def shape(dims, kind):
    return jax.ShapeDtypeStruct(tuple(dims), kind)


def run(kernel, outs, ins, scratch=(), flops=0, limit=24, scalars=0, name=None):
    moved = sum(a.size * a.dtype.itemsize for a in ins) + sum(o.size * jnp.dtype(o.dtype).itemsize for o in outs)
    spaces = [pl.BlockSpec(memory_space=pltpu.SMEM)] * scalars
    spaces += [pl.BlockSpec(memory_space=pltpu.VMEM)] * (len(ins) - scalars)
    return pl.pallas_call(
        kernel,
        out_shape=tuple(outs),
        in_specs=spaces,
        out_specs=tuple(pl.BlockSpec(memory_space=pltpu.VMEM) for _ in outs),
        scratch_shapes=list(scratch),
        compiler_params=pltpu.CompilerParams(vmem_limit_bytes=limit << 20),
        cost_estimate=pl.CostEstimate(flops=flops, bytes_accessed=moved, transcendentals=0),
        name=name,
    )(*ins)


def dot(left, right):
    return lax.dot_general(left, right, (((1,), (0,)), ((), ())), preferred_element_type=WIDE)


def dot_columns(left, right):
    return lax.dot_general(left, right, (((1,), (1,)), ((), ())), preferred_element_type=WIDE)


def send(values, axis, bit):
    size = lax.axis_size(axis)
    return lax.ppermute(values, axis, [(i, i ^ bit) for i in range(size)])


def after(value, *earlier):
    return lax.optimization_barrier((value,) + earlier)[0]


def halves(rows):
    middle = rows.shape[0] // 2
    return (rows[:middle], rows[middle:])


def gather_rows(shard):
    size = lax.axis_size("dp")
    if size == 8:
        from_x = send(shard, "dp", 2)
        from_y = send(shard, "dp", 4)
        first = send(halves(from_x)[0], "dp", 4)
        second = send(halves(from_y)[1], "dp", 2)
        own = [shard, from_x, from_y, first, second]
    else:
        joined = shard
        bit = 2
        while bit < size:
            joined = jnp.concatenate([joined, send(joined, "dp", bit)], axis=0)
            bit *= 2
        own = [joined]
    return own + [send(piece, "dp", 1) for piece in own]


def scatter_near(own, other):
    return own + send(other, "dp", 1).astype(WIDE)


def scatter_far(own):
    size = lax.axis_size("dp")
    if size == 8:
        here, to_x, to_y, far = jnp.split(own, 4, axis=0)
        far_x, far_y = halves(far.astype(LOW))
        by_x = send(far_x, "dp", 2).astype(WIDE)
        by_y = send(far_y, "dp", 4).astype(WIDE)
        x_low, x_high = halves(to_x)
        y_low, y_high = halves(to_y)
        to_x = jnp.concatenate([x_low.astype(LOW), (x_high + by_y).astype(LOW)], axis=0)
        to_y = jnp.concatenate([(y_low + by_x).astype(LOW), y_high.astype(LOW)], axis=0)
        return (here, send(to_x, "dp", 2), send(to_y, "dp", 4))
    bit = size // 2
    while bit > 1:
        low, high = halves(own)
        received = send(high.astype(LOW), "dp", bit)
        if bit == 2:
            return (low, received, jnp.zeros_like(received))
        own = low + received.astype(WIDE)
        bit //= 2
    return (own, jnp.zeros_like(own, LOW), jnp.zeros_like(own, LOW))


def block_order(size):
    return [2 * i for i in range(size // 2)] + [2 * i + 1 for i in range(size // 2)]


def xor_blocks(blocks, index):
    bit = 1
    while bit < len(blocks):
        taken = (index & bit) != 0
        blocks = [jnp.where(taken, blocks[i ^ bit], blocks[i]) for i in range(len(blocks))]
        bit *= 2
    return blocks


def to_relative(rows):
    size = lax.axis_size("dp")
    blocks = xor_blocks(jnp.split(rows, size, axis=-1), lax.axis_index("dp"))
    return jnp.concatenate([blocks[i] for i in block_order(size)], axis=-1)


def to_absolute(rows):
    size = lax.axis_size("dp")
    order = block_order(size)
    blocks = jnp.split(rows, size, axis=-1)
    blocks = xor_blocks([blocks[order.index(i)] for i in range(size)], lax.axis_index("dp"))
    return jnp.concatenate(blocks, axis=-1)


def gather_tokens(rows):
    return [rows] + [send(rows, "tensor", k) for k in range(1, lax.axis_size("tensor"))]


def scatter_tokens(parts):
    return [parts[0]] + [send(parts[k], "tensor", k) for k in range(1, len(parts))]


def sum_tensor(values):
    total = values
    for k in range(1, lax.axis_size("tensor")):
        total = total + send(values, "tensor", k)
    return total


def sum_all(values):
    for axis in ("dp", "tensor"):
        bit = 1
        while bit < lax.axis_size(axis):
            values = values + send(values, axis, bit)
            bit *= 2
    return values


def gather_small(values):
    size = lax.axis_size("dp")
    index = lax.axis_index("dp")
    place = lax.broadcasted_iota(jnp.int32, (size, values.shape[0]), 0) == index
    full = jnp.where(place, values[None, :], jnp.zeros_like(values)[None, :])
    bit = 1
    while bit < size:
        full = full + send(full, "dp", bit)
        bit *= 2
    return full


def assemble(target, pieces):
    row = 0
    for piece in pieces:
        target[row : row + piece.shape[0], :] = piece[...]
        row += piece.shape[0]


def tiles(extent, body, tile=TILE):
    if extent <= tile or extent % tile:
        body(0, extent)
        return

    def step(i, carry):
        body(pl.multiple_of(i * tile, tile), tile)
        return carry

    lax.fori_loop(0, extent // tile, step, 0)


def project_back(left, right, outs):
    count = outs[0].shape[0]

    def body(at, width):
        product = dot_columns(left[...], right[pl.ds(at, width), :])
        for k, out in enumerate(outs):
            out[:, pl.ds(at, width)] = product[k * count : (k + 1) * count].astype(out.dtype)

    tiles(right.shape[0], body)


def rows_transposed_dot(rows_t, grads, own, other, at_out):
    half = own.shape[0]

    def body(at, width):
        columns = grads[:, pl.ds(at, width)]
        place = pl.ds(at_out + at, width)
        own[:, place] = dot(rows_t[:half, :], columns)
        other[:, place] = dot(rows_t[half:, :], columns).astype(LOW)

    tiles(grads.shape[1], body)


def transpose_into(target, pieces):
    column = 0
    for piece in pieces:
        target[:, column : column + piece.shape[0]] = piece[...].T
        column += piece.shape[0]


def prepare_shards(gain_one, gain_two, query, key, value, output, gate, up, down):
    widths = (query.shape[1], key.shape[1], value.shape[1])
    hidden = gate.shape[1]

    def kernel(g1, g2, q, k, v, o, g, u, d, in_out, out_out, feed_out, down_out):
        first, second = g1[...], g2[...]
        at = 0
        for ref, width in zip((q, k, v), widths, strict=True):
            in_out[:, at : at + width] = (ref[...].astype(WIDE) * first).astype(LOW)
            at += width
        out_out[...] = o[...].T
        feed_out[:, :hidden] = (g[...].astype(WIDE) * second).astype(LOW)
        feed_out[:, hidden:] = (u[...].astype(WIDE) * second).astype(LOW)
        down_out[...] = d[...].T

    rows = query.shape[0]
    outs = [
        shape((rows, sum(widths)), LOW),
        shape((rows, output.shape[0]), LOW),
        shape((rows, 2 * hidden), LOW),
        shape((rows, down.shape[0]), LOW),
    ]
    return run(kernel, outs, [gain_one, gain_two, query, key, value, output, gate, up, down], name="prepare_shards")


def first_norm(index, block_input, out_grad):
    size = lax.axis_size("dp")
    width = block_input.shape[1] // size
    direct = width % 128 == 0
    if not direct:
        block_input, out_grad = to_relative(block_input), to_relative(out_grad)

    def kernel(at, x, g, x_out, g_out, normed_out):
        if direct:
            for j, block in enumerate(block_order(size)):
                place = pl.ds(pl.multiple_of((at[0] ^ block) * width, width), width)
                x_out[:, j * width : (j + 1) * width] = x[:, place]
                g_out[:, j * width : (j + 1) * width] = g[:, place]
        else:
            x_out[...], g_out[...] = x[...], g[...]
        rows = x_out[...].astype(WIDE)
        inverse = lax.rsqrt(jnp.mean(rows * rows, axis=-1, keepdims=True) + EPSILON)
        normed_out[...] = (rows * inverse).astype(LOW)

    outs = [shape(block_input.shape, LOW)] * 3
    return run(kernel, outs, [index, block_input, out_grad], scalars=1, name="first_norm")


def middle_norm(x, parts):
    def kernel(x_ref, *refs):
        total = x_ref[...].astype(WIDE)
        for ref in refs[: len(parts)]:
            total = total + ref[...].astype(WIDE)
        middle, normed = refs[len(parts) :]
        middle[...] = total
        inverse = lax.rsqrt(jnp.mean(total * total, axis=-1, keepdims=True) + EPSILON)
        normed[...] = (total * inverse).astype(LOW)

    return run(kernel, [shape(x.shape, WIDE), shape(x.shape, LOW)], [x, *parts], name="middle_norm")


def back_through_norm(rows, scaled):
    inverse = lax.rsqrt(jnp.mean(rows * rows, axis=-1, keepdims=True) + EPSILON)
    normed = rows * inverse
    inner = jnp.mean(scaled * normed, axis=-1, keepdims=True)
    return inverse * (scaled - normed * inner)


def middle_back(grads, middle, parts):
    def kernel(g, m, *refs):
        scaled = refs[0][...]
        for ref in refs[1 : len(parts)]:
            scaled = scaled + ref[...].astype(WIDE)
        wide, low = refs[len(parts) :]
        total = g[...].astype(WIDE) + back_through_norm(m[...], scaled)
        wide[...] = total
        low[...] = total.astype(LOW)

    outs = [shape(middle.shape, WIDE), shape(middle.shape, LOW)]
    return run(kernel, outs, [grads, middle, *parts], name="middle_back")


def store_absolute(index, out, values):
    size = lax.axis_size("dp")
    width = values.shape[1] // size
    for j, block in enumerate(block_order(size)):
        place = pl.ds(pl.multiple_of((index ^ block) * width, width), width)
        out[:, place] = values[:, j * width : (j + 1) * width]


def last_back(index, middle_grad, x, parts):
    direct = (x.shape[1] // lax.axis_size("dp")) % 128 == 0

    def kernel(at, m, x_ref, *refs):
        scaled = refs[0][...]
        for ref in refs[1 : len(parts)]:
            scaled = scaled + ref[...].astype(WIDE)
        total = m[...] + back_through_norm(x_ref[...].astype(WIDE), scaled)
        if direct:
            store_absolute(at[0], refs[-1], total)
        else:
            refs[-1][...] = total

    (out,) = run(kernel, [shape(x.shape, WIDE)], [index, middle_grad, x, *parts], scalars=1, name="last_back")
    return out if direct else to_absolute(out)


def block_sum(index, middle, parts):
    direct = (middle.shape[1] // lax.axis_size("dp")) % 128 == 0

    def kernel(at, m, *refs):
        total = m[...]
        for ref in refs[: len(parts)]:
            total = total + ref[...].astype(WIDE)
        if direct:
            store_absolute(at[0], refs[-1], total.astype(LOW))
        else:
            refs[-1][...] = total.astype(LOW)

    (out,) = run(kernel, [shape(middle.shape, LOW)], [index, middle, *parts], scalars=1, name="block_sum")
    return out if direct else to_absolute(out)


def attention(rows, in_pieces, out_pieces, gains, cosine, sine, row_at, column_at, dims):
    query_width, key_width, head_dim = dims
    local, features = rows[0].shape
    length = local * len(rows)
    width = query_width + 2 * key_width
    heads, kv_heads = query_width // head_dim, key_width // head_dim
    group = heads // kv_heads
    scale = head_dim ** (-0.5)
    ranks = len(rows)

    def kernel(*refs):
        refs = list(refs)
        row_refs = [refs.pop(0) for _ in rows]
        in_refs = [refs.pop(0) for _ in in_pieces]
        out_refs = [refs.pop(0) for _ in out_pieces]
        gain, cos, sin, q_at, k_at = (refs.pop(0) for _ in range(5))
        raw, rotated, values, attended, lse = (refs.pop(0) for _ in range(5))
        parts = [refs.pop(0) for _ in range(ranks)]
        all_rows, weights, out_weights = refs
        assemble(all_rows, row_refs)
        assemble(weights, in_refs)
        assemble(out_weights, out_refs)

        def project(at, size):
            raw[:, pl.ds(at, size)] = dot(all_rows[...], weights[:, pl.ds(at, size)])

        tiles(query_width + key_width, project)
        for at in range(0, key_width, min(TILE, key_width)):
            size = min(TILE, key_width)
            start = query_width + key_width + at
            values[:, at : at + size] = dot(all_rows[...], weights[:, start : start + size]).astype(LOW)

        def prepare(h, carry):
            place = pl.ds(pl.multiple_of(h * head_dim, head_dim), head_dim)
            head = raw[:, place]
            inverse = lax.rsqrt(jnp.mean(head * head, axis=-1, keepdims=True) + EPSILON)
            which = jnp.where(h < heads, gain[0:1, :], gain[1:2, :])
            scaled = head * inverse * which
            rotated[:, place] = (scaled * cos[...] + pltpu.roll(scaled, head_dim // 2, 1) * sin[...]).astype(LOW)
            return carry

        lax.fori_loop(0, heads + kv_heads, prepare, 0)

        def attend(i, carry):
            h, b = i // ranks, i % ranks
            place = pl.ds(pl.multiple_of(h * head_dim, head_dim), head_dim)
            kv = h // group
            key_place = pl.ds(pl.multiple_of(query_width + kv * head_dim, head_dim), head_dim)
            value_place = pl.ds(pl.multiple_of(kv * head_dim, head_dim), head_dim)
            block = pl.ds(pl.multiple_of(b * local, local), local)
            scores = dot_columns(rotated[block, place], rotated[:, key_place]) * scale
            scores = jnp.where(q_at[block, :] >= k_at[...], scores, HIDDEN_FAR)
            top = jnp.max(scores, axis=-1, keepdims=True)
            weight = jnp.exp(scores - top)
            total = jnp.sum(weight, axis=-1, keepdims=True)
            probs = (weight * (1.0 / total)).astype(LOW)
            attended[block, place] = dot(probs, values[:, value_place]).astype(LOW)
            lse[block, place] = jnp.broadcast_to(top + jnp.log(total), (local, head_dim))
            return carry

        lax.fori_loop(0, heads * ranks, attend, 0)
        project_back(attended, out_weights, parts)

    outs = [
        shape((length, query_width + key_width), WIDE),
        shape((length, query_width + key_width), LOW),
        shape((length, key_width), LOW),
        shape((length, query_width), LOW),
        shape((length, query_width), WIDE),
        shape((local, features), WIDE),
    ] + [shape((local, features), LOW)] * (ranks - 1)
    scratch = [
        pltpu.VMEM((length, features), LOW),
        pltpu.VMEM((features, width), LOW),
        pltpu.VMEM((features, query_width), LOW),
    ]
    flops = 2 * length * features * (width + query_width) + 4 * length * length * query_width
    ins = [*rows, *in_pieces, *out_pieces, gains, cosine, sine, row_at, column_at]
    return run(kernel, outs, ins, scratch, flops, name="attention")


def attention_back(rows, in_pieces, out_pieces, saved, gains, cosine, sine, row_at, column_at, dims):
    query_width, key_width, head_dim = dims
    local, features = rows[0].shape
    length = local * len(rows)
    width = query_width + 2 * key_width
    heads, kv_heads = query_width // head_dim, key_width // head_dim
    group = heads // kv_heads
    scale = head_dim ** (-0.5)
    ranks = len(rows)

    def kernel(*refs):
        refs = list(refs)
        row_refs = [refs.pop(0) for _ in rows]
        in_refs = [refs.pop(0) for _ in in_pieces]
        out_refs = [refs.pop(0) for _ in out_pieces]
        raw, rotated, values, attended, lse = (refs.pop(0) for _ in range(5))
        gain, cos, sin, q_at, k_at = (refs.pop(0) for _ in range(5))
        grads, gain_grads = refs.pop(0), refs.pop(0)
        parts = [refs.pop(0) for _ in range(ranks)]
        all_rows, weights, out_weights, grad_attended, grad_query, grad_key, grad_value = refs
        assemble(all_rows, row_refs)
        assemble(weights, in_refs)
        assemble(out_weights, out_refs)

        def project(at, size):
            grad_attended[:, pl.ds(at, size)] = dot(all_rows[...], out_weights[:, pl.ds(at, size)]).astype(LOW)

        tiles(query_width, project)
        grad_key[...] = jnp.zeros_like(grad_key)
        grad_value[...] = jnp.zeros_like(grad_value)

        def attend(i, carry):
            h, b = i // ranks, i % ranks
            place = pl.ds(pl.multiple_of(h * head_dim, head_dim), head_dim)
            kv = h // group
            key_place = pl.ds(pl.multiple_of(query_width + kv * head_dim, head_dim), head_dim)
            value_place = pl.ds(pl.multiple_of(kv * head_dim, head_dim), head_dim)
            block = pl.ds(pl.multiple_of(b * local, local), local)
            query, upper = rotated[block, place], grad_attended[block, place]
            keys = rotated[:, key_place]
            scores = dot_columns(query, keys) * scale
            probs = jnp.where(q_at[block, :] >= k_at[...], jnp.exp(scores - lse[block, place][:, :1]), 0.0)
            delta = jnp.sum(upper.astype(WIDE) * attended[block, place].astype(WIDE), axis=-1, keepdims=True)
            grad_probs = dot_columns(upper, values[:, value_place])
            grad_scores = (probs * (grad_probs - delta) * scale).astype(LOW)
            grad_query[block, place] = dot(grad_scores, keys)
            grad_key[:, value_place] += lax.dot_general(
                grad_scores, query, (((0,), (0,)), ((), ())), preferred_element_type=WIDE
            )
            grad_value[:, value_place] += lax.dot_general(
                probs.astype(LOW), upper, (((0,), (0,)), ((), ())), preferred_element_type=WIDE
            )
            return carry

        lax.fori_loop(0, heads * ranks, attend, 0)

        def back(raw_at, source, source_at, which):
            place = pl.ds(pl.multiple_of(raw_at, head_dim), head_dim)
            head = raw[:, place]
            inverse = lax.rsqrt(jnp.mean(head * head, axis=-1, keepdims=True) + EPSILON)
            hat = head * inverse
            upper = source[:, pl.ds(pl.multiple_of(source_at, head_dim), head_dim)]
            normed = upper * cos[...] + pltpu.roll(upper * sin[...], head_dim // 2, 1)
            scaled = normed * gain[which : which + 1, :]
            inner = jnp.mean(scaled * hat, axis=-1, keepdims=True)
            grads[:, place] = (inverse * (scaled - hat * inner)).astype(LOW)
            return jnp.sum(normed * hat, axis=0, keepdims=True)

        zero = jnp.zeros((1, head_dim), WIDE)
        gain_grads[0:1, :] = lax.fori_loop(
            0, heads, lambda h, total: total + back(h * head_dim, grad_query, h * head_dim, 0), zero
        )
        gain_grads[1:2, :] = lax.fori_loop(
            0, kv_heads, lambda h, total: total + back(query_width + h * head_dim, grad_key, h * head_dim, 1), zero
        )
        grads[:, query_width + key_width :] = grad_value[...].astype(LOW)
        project_back(grads, weights, parts)

    outs = [
        shape((length, width), LOW),
        shape((2, head_dim), WIDE),
        shape((local, features), WIDE),
    ] + [shape((local, features), LOW)] * (ranks - 1)
    scratch = [
        pltpu.VMEM((length, features), LOW),
        pltpu.VMEM((features, width), LOW),
        pltpu.VMEM((features, query_width), LOW),
        pltpu.VMEM((length, query_width), LOW),
        pltpu.VMEM((length, query_width), WIDE),
        pltpu.VMEM((length, key_width), WIDE),
        pltpu.VMEM((length, key_width), WIDE),
    ]
    flops = 2 * length * features * (width + query_width) + 10 * length * length * query_width
    ins = [*rows, *in_pieces, *out_pieces, *saved, gains, cosine, sine, row_at, column_at]
    return run(kernel, outs, ins, scratch, flops, name="attention_back")


def feed(rows, grad_rows, feed_pieces, down_pieces):
    local, features = rows[0].shape
    ranks = len(rows)
    length = local * ranks
    hidden = down_pieces[0].shape[1]

    def kernel(*refs):
        refs = list(refs)
        row_refs = [refs.pop(0) for _ in rows]
        grad_refs = [refs.pop(0) for _ in grad_rows]
        feed_refs = [refs.pop(0) for _ in feed_pieces]
        down_refs = [refs.pop(0) for _ in down_pieces]
        mixed, grads = refs.pop(0), refs.pop(0)
        parts = [refs.pop(0) for _ in range(ranks)]
        all_rows, all_grads, weights, down_weights = refs
        assemble(all_rows, row_refs)
        assemble(all_grads, grad_refs)
        assemble(weights, feed_refs)
        assemble(down_weights, down_refs)

        def body(at, size):
            place = pl.ds(at, size)
            second = pl.ds(hidden + at, size)
            gate = dot(all_rows[...], weights[:, place])
            up = dot(all_rows[...], weights[:, second])
            upper = dot(all_grads[...], down_weights[:, place])
            sigmoid = 1.0 / (1.0 + jnp.exp(-gate))
            silu = gate * sigmoid
            mixed[:, place] = (silu * up).astype(LOW)
            grads[:, place] = (upper * up * (sigmoid * (1.0 + gate * (1.0 - sigmoid)))).astype(LOW)
            grads[:, second] = (upper * silu).astype(LOW)

        tiles(hidden, body)
        project_back(grads, weights, parts)

    outs = [
        shape((length, hidden), LOW),
        shape((length, 2 * hidden), LOW),
        shape((local, features), WIDE),
    ] + [shape((local, features), LOW)] * (ranks - 1)
    scratch = [
        pltpu.VMEM((length, features), LOW),
        pltpu.VMEM((length, features), LOW),
        pltpu.VMEM((features, 2 * hidden), LOW),
        pltpu.VMEM((features, hidden), LOW),
    ]
    ins = [*rows, *grad_rows, *feed_pieces, *down_pieces]
    return run(kernel, outs, ins, scratch, 10 * length * features * hidden, name="feed")


def feed_out(mixed, down_pieces, ranks):
    length, hidden = mixed.shape
    features = sum(piece.shape[0] for piece in down_pieces)
    local = length // ranks

    def kernel(mixed_ref, *refs):
        pieces, parts, weights = refs[: len(down_pieces)], refs[len(down_pieces) : -1], refs[-1]
        assemble(weights, pieces)
        project_back(mixed_ref, weights, parts)

    outs = [shape((local, features), WIDE)] + [shape((local, features), LOW)] * (ranks - 1)
    scratch = [pltpu.VMEM((features, hidden), LOW)]
    return run(kernel, outs, [mixed, *down_pieces], scratch, 2 * length * features * hidden, name="feed_out")


def weight_grads(first_rows, first_grads, second_rows, second_grads):
    local, features = first_rows[0].shape
    length = local * len(first_rows)
    widths = (first_grads.shape[1], second_grads.shape[1])

    def kernel(*refs):
        refs = list(refs)
        one = [refs.pop(0) for _ in first_rows]
        two = [refs.pop(0) for _ in second_rows]
        first, second, own, other, turned = refs
        transpose_into(turned, one)
        rows_transposed_dot(turned, first, own, other, 0)
        transpose_into(turned, two)
        rows_transposed_dot(turned, second, own, other, widths[0])

    half = features // 2
    outs = [shape((half, sum(widths)), WIDE), shape((half, sum(widths)), LOW)]
    scratch = [pltpu.VMEM((features, length), LOW)]
    ins = [*first_rows, *second_rows, first_grads, second_grads]
    return run(kernel, outs, ins, scratch, 2 * length * features * sum(widths), name="weight_grads")


def finish(terms, gain, weights, turned):
    rows = terms[0].shape[0]

    def kernel(*refs):
        refs = list(refs)
        here, by_x, by_y, gain_ref = (refs.pop(0) for _ in range(4))
        weight_refs = [refs.pop(0) for _ in weights]
        outs = [refs.pop(0) for _ in weights]
        last, sums = refs
        at = 0
        total = jnp.zeros((rows, 1), WIDE)
        for weight, out in zip(weight_refs, outs, strict=True):
            place = slice(at, at + weight.shape[1])
            value = here[:, place] + by_x[:, place].astype(WIDE) + by_y[:, place].astype(WIDE)
            out[...] = value * gain_ref[...]
            total = total + jnp.sum(value * weight[...].astype(WIDE), axis=1, keepdims=True)
            at += weight.shape[1]
        rest = slice(at, at + turned)
        last[...] = (here[:, rest] + by_x[:, rest].astype(WIDE) + by_y[:, rest].astype(WIDE)).T
        sums[...] = jnp.broadcast_to(total, sums.shape)

    outs = [shape((rows, w.shape[1]), WIDE) for w in weights] + [shape((turned, rows), WIDE), shape((rows, 128), WIDE)]
    return run(kernel, outs, [*terms, gain, *weights], name="finish")


def body(
    block_input,
    first_gain,
    query_gain,
    key_gain,
    query_weight,
    key_matrix,
    value_matrix,
    output_weight,
    second_gain,
    gate_weight,
    up_weight,
    down_weight,
    out_grad,
):
    ranks = lax.axis_size("tensor")
    rank = lax.axis_index("tensor")
    dp_size = lax.axis_size("dp")
    dp_index = lax.axis_index("dp")
    index = dp_index.astype(jnp.int32).reshape(1)
    local = block_input.shape[0]
    length = local * ranks
    small = query_gain.shape[0]
    head_dim = small * dp_size
    dims = (query_weight.shape[1], key_matrix.shape[1], head_dim)

    gain_one = first_gain.astype(WIDE)[:, None]
    gain_two = second_gain.astype(WIDE)[:, None]
    in_shard, out_shard, feed_shard, down_shard = prepare_shards(
        gain_one, gain_two, query_weight, key_matrix, value_matrix, output_weight, gate_weight, up_weight, down_weight
    )
    in_pieces = gather_rows(in_shard)
    input_rows, grad_local, normed_one = first_norm(index, block_input, out_grad)
    rows_one = gather_tokens(normed_one)
    gains = gather_small(jnp.concatenate([query_gain, key_gain])).astype(WIDE)
    gains = jnp.stack([gains[:, :small].reshape(-1), gains[:, small:].reshape(-1)])
    out_pieces = gather_rows(out_shard)

    slot = lax.broadcasted_iota(jnp.int32, (ranks, local), 0)
    within = lax.broadcasted_iota(jnp.int32, (ranks, local), 1)
    position = ((slot ^ rank) * local + within).reshape(length)
    half = head_dim // 2
    freqs = THETA ** (-(jnp.arange(half, dtype=WIDE) * (2.0 / head_dim)))
    angles = position.astype(WIDE)[:, None] * freqs[None, :]
    cosine, sine = jnp.cos(angles), jnp.sin(angles)
    cosine = jnp.concatenate([cosine, cosine], axis=1)
    sine = jnp.concatenate([-sine, sine], axis=1)
    row_at, column_at = position[:, None], position[None, :]
    tables = (gains, cosine, sine, row_at, column_at)

    late = lax.optimization_barrier((grad_local, feed_shard, down_shard, tuple(rows_one), tuple(in_pieces)))
    grad_rows = gather_tokens(late[0])
    feed_pieces = gather_rows(late[1])
    down_pieces = gather_rows(late[2])
    results = attention(rows_one, in_pieces, out_pieces, *tables, dims)
    saved, parts = results[:-ranks], scatter_tokens(results[-ranks:])
    parts = lax.optimization_barrier((tuple(parts), tuple(feed_pieces), tuple(down_pieces), tuple(grad_rows)))[0]
    middle, normed_two = middle_norm(input_rows, parts)
    rows_two = gather_tokens(normed_two)
    mixed, grad_hidden, *parts = feed(rows_two, grad_rows, feed_pieces, down_pieces)
    scaled_two = scatter_tokens(parts)
    feed_own, feed_other = weight_grads(rows_two, grad_hidden, grad_rows, mixed)
    feed_near = scatter_near(feed_own, feed_other)
    scaled_two = lax.optimization_barrier((tuple(scaled_two), feed_near))[0]
    middle_grad, grad_attn = middle_back(grad_local, middle, scaled_two)
    attn_rows = gather_tokens(grad_attn)
    feed_terms = scatter_far(feed_near)
    block_parts = feed_out(mixed, down_pieces, ranks)
    attn_rows, block_parts = lax.optimization_barrier((tuple(attn_rows), tuple(block_parts)))
    block_parts = scatter_tokens(block_parts)
    grad_in, head_gains, *parts = attention_back(attn_rows, in_pieces, out_pieces, saved, *tables, dims)
    parts, attn_rows, grad_in, head_gains = lax.optimization_barrier(
        (tuple(parts), attn_rows, grad_in, head_gains, tuple(block_parts), feed_terms)
    )[:4]
    scaled_one = scatter_tokens(parts)
    in_terms = scatter_far(scatter_near(*weight_grads(rows_one, grad_in, attn_rows, saved[3])))
    block_output = block_sum(index, middle, block_parts)
    gate_grad, up_grad, down_grad, second_sums = finish(feed_terms, gain_two, (gate_weight, up_weight), down_weight.shape[0])
    second_gain_grad = sum_tensor(second_sums[:, 0])
    head_gains = sum_all(head_gains)
    query_gain_grad = lax.dynamic_slice(head_gains[0], (dp_index * small,), (small,))
    key_gain_grad = lax.dynamic_slice(head_gains[1], (dp_index * small,), (small,))
    input_grad = last_back(index, middle_grad, input_rows, scaled_one)
    query_grad, key_grad, value_grad, output_grad, first_sums = finish(
        in_terms, gain_one, (query_weight, key_matrix, value_matrix), output_weight.shape[0]
    )
    first_gain_grad = sum_tensor(first_sums[:, 0])
    return (
        block_output,
        input_grad,
        first_gain_grad,
        query_gain_grad,
        key_gain_grad,
        query_grad,
        key_grad,
        value_grad,
        output_grad,
        second_gain_grad,
        gate_grad,
        up_grad,
        down_grad,
    )


def solution(mesh):
    tokens = P(("dp", "tensor"), None)
    vector = P("dp")
    rows = P("dp", "tensor")
    columns = P("tensor", "dp")
    return jax.shard_map(
        body,
        mesh=mesh,
        in_specs=(tokens, vector, vector, vector, rows, rows, rows, columns, vector, rows, rows, columns, tokens),
        out_specs=(tokens, tokens, vector, vector, vector, rows, rows, rows, columns, vector, rows, rows, columns),
        check_vma=False,
    )
```
